32 devices in a mesh: req: 4 (over x, core), seq: 8 (over z, y).
Axes of the slice: x: 2, y: 2, z: 4, core: 2. Of those that a mesh axis runs over, the one named last changes fastest.
Arguments:
- query_nope: bfloat16 [8, 2, 128, 128], P('req', None, 'seq'), may hold values from -12 to 12
- query_rope: bfloat16 [8, 2, 8192], P('req', None, 'seq'), may hold values from -32 to 32
- key_absorb: bfloat16 [128, 128, 512], P('seq'), may hold values from -0.5 to 0.5
- value_up_matrix: bfloat16 [128, 512, 128], P('seq'), may hold values from -0.5 to 0.5
- latent_cache: bfloat16 [8, 32768, 512], P('req', 'seq'), may hold values from -6 to 6
- rope_cache: bfloat16 [8, 64, 32768], P('req', None, 'seq'), may hold values from -4 to 4
- new_latent: bfloat16 [8, 2, 512], P('req'), may hold values from -12 to 12
- new_rope: bfloat16 [8, 2, 64], P('req'), may hold values from -10 to 10
- lengths: int32 [8], P('req'), may hold values from 1 to 32768
- positions: int32 [8, 2], P('req'), may hold values from 0 to 8191
Outputs:
- head_outputs: bfloat16 [8, 2, 128, 128], P('req', None, 'seq')
The draws below stay inside these ranges and needn't reach their ends.
All inputs are finite; a program needn't handle non-finite values.
Results may differ from the reference program's by a relative error of at most 0.0087.
Values may be sent and summed in bfloat16 or wider, within the bound.
No kernel may reach another device: no remote copies, remote signals or barrier semaphores. Data moves between devices by JAX's collectives and lax.ppermute only.
A program may use at most 64 MiB of HBM per device.

```python
import jax
import jax.numpy as jnp
from jax import lax

H = 128
KVL = 512
ROPE = 64
NOPE = 128
VH = 128
STEPS = 2
REQUESTS = 8
CTX = 32768


def rope_pair(key):
    query_start_offset = jnp.clip(jax.random.normal(jax.random.fold_in(key, 101), (REQUESTS, STEPS, H, ROPE), jnp.float32), -4.0, 4.0)
    key_start_offset = jnp.clip(jax.random.normal(jax.random.fold_in(key, 102), (REQUESTS, ROPE, CTX), jnp.float32), -4.0, 4.0)
    return (query_start_offset.reshape(REQUESTS, STEPS, H * ROPE), key_start_offset)


def draw_query_rope(key, part):
    return rope_pair(key)[0].astype(jnp.bfloat16)


def draw_rope_cache(key, part):
    return rope_pair(key)[1].astype(jnp.bfloat16)


def set_ends(drawn, rng, low, largest):
    longest = drawn.shape.index(max(drawn.shape))
    spots = []
    for shift in (0, 1):
        where = [jax.random.randint(jax.random.fold_in(rng, axis), (), 0, length) for axis, length in enumerate(drawn.shape)]
        where[longest] = (where[longest] + shift) % drawn.shape[longest]
        spots.append(tuple(where))
    return drawn.at[spots[0]].set(low).at[spots[1]].set(largest)


def level_of(rng, dims, cuts, least, largest):
    factor_of, own = 1.0, jax.random.fold_in(rng, 6)
    for position, shards_of in cuts:
        steps = jnp.exp(jax.random.uniform(jax.random.fold_in(own, position), (shards_of,), jnp.float32, least / len(cuts), largest / len(cuts)))
        factor_of = factor_of * jnp.repeat(steps, dims[position] // shards_of).reshape([-1 if axis == position else 1 for axis in range(len(dims))])
    return factor_of


def noise(own_key, dims, spread, bound, split=(), kind=jnp.bfloat16):
    entries = jax.random.normal(own_key, dims, jnp.float32) * spread
    if len(split) > 0:
        entries = level_of(own_key, dims, split, -0.22, 0.18) * entries
    return jnp.clip(entries, min=-bound, max=bound).astype(kind)


def setup_inputs(seed: int = 0) -> dict:
    streams_of = jax.random.split(jax.random.key(seed), 11)
    query_nope = noise(streams_of[0], (REQUESTS, STEPS, H, NOPE), 2.0, 12.0, ((0, 4), (2, 8)))
    query_rope = draw_query_rope(jax.random.fold_in(streams_of[10], 71), 0)
    key_absorb = noise(streams_of[2], (H, NOPE, KVL), NOPE ** -0.5, 0.5, ((0, 8),))
    value_up_matrix = noise(streams_of[3], (H, KVL, VH), (KVL // 4) ** -0.5, 0.5, ((0, 8),))
    latent_cache = noise(streams_of[4], (REQUESTS, CTX, KVL), 1.0, 6.0, ((0, 4), (1, 8)))
    rope_cache = draw_rope_cache(jax.random.fold_in(streams_of[10], 71), 0)
    new_latent = noise(streams_of[6], (REQUESTS, STEPS, KVL), 2.5, 12.0, ((0, 4),))
    new_rope = noise(streams_of[7], (REQUESTS, STEPS, ROPE), 2.0, 10.0, ((0, 4),))
    lengths = set_ends(jax.random.randint(streams_of[8], (REQUESTS,), 1, CTX + 1), jax.random.fold_in(streams_of[8], 1), 1, CTX).astype(jnp.int32)
    positions = set_ends(jax.random.randint(streams_of[9], (REQUESTS, STEPS), 0, 8192), jax.random.fold_in(streams_of[9], 1), 0, 8191).astype(jnp.int32)
    return dict(query_nope=query_nope, query_rope=query_rope, key_absorb=key_absorb, value_up_matrix=value_up_matrix, latent_cache=latent_cache, rope_cache=rope_cache, new_latent=new_latent, new_rope=new_rope, lengths=lengths, positions=positions)


NEG_FILL = -1e30


def rotate(vectors, where_at):
    half_width = vectors.shape[-1] // 2
    frequency = 10000.0 ** (-jnp.arange(half_width, dtype=jnp.float32) / half_width)
    angles = where_at.astype(jnp.float32)[..., None] * frequency
    leading = vectors[..., :half_width].astype(jnp.float32)
    trailing = vectors[..., half_width:].astype(jnp.float32)
    return jnp.concatenate([leading * jnp.cos(angles) - trailing * jnp.sin(angles), leading * jnp.sin(angles) + trailing * jnp.cos(angles)], axis=-1)


def reference(query_nope, query_rope, key_absorb, value_up_matrix, latent_cache, rope_cache, new_latent, new_rope, lengths, positions):
    softmax_scale = (NOPE + ROPE) ** -0.5
    query_latent = jnp.einsum('rshn,hnk->rshk', query_nope.astype(jnp.float32), key_absorb.astype(jnp.float32)).astype(jnp.bfloat16)
    query_rotary = query_rope.reshape(REQUESTS, STEPS, H, ROPE)
    key_new = rotate(new_rope, positions).astype(jnp.bfloat16)
    causal = jnp.arange(STEPS)[None, :] <= jnp.arange(STEPS)[:, None]

    def one_request(items):
        latent_query, rotary_query, cached, rotary_cached, latent_new, rotary_new, length = items
        is_valid_entry = jnp.arange(CTX) < length
        cache_score = (jnp.einsum('shk,tk->sht', latent_query.astype(jnp.float32), cached.astype(jnp.float32)) + jnp.einsum('shd,dt->sht', rotary_query.astype(jnp.float32), rotary_cached.astype(jnp.float32))) * softmax_scale
        cache_score = jnp.where(is_valid_entry[None, None, :], cache_score, NEG_FILL)
        new_score = (jnp.einsum('shk,jk->shj', latent_query.astype(jnp.float32), latent_new.astype(jnp.float32)) + jnp.einsum('shd,jd->shj', rotary_query.astype(jnp.float32), rotary_new.astype(jnp.float32))) * softmax_scale
        new_score = jnp.where(causal[:, None, :], new_score, NEG_FILL)
        highest = jnp.maximum(jnp.max(cache_score, axis=-1), jnp.max(new_score, axis=-1))
        cache_weight = jnp.where(is_valid_entry[None, None, :], jnp.exp(cache_score - highest[..., None]), 0.0)
        new_weight = jnp.where(causal[:, None, :], jnp.exp(new_score - highest[..., None]), 0.0)
        total = jnp.sum(cache_weight, axis=-1) + jnp.sum(new_weight, axis=-1)
        mixed = jnp.einsum('sht,tk->shk', cache_weight.astype(jnp.bfloat16).astype(jnp.float32), cached.astype(jnp.float32))
        mixed = mixed + jnp.einsum('shj,jk->shk', new_weight.astype(jnp.bfloat16).astype(jnp.float32), latent_new.astype(jnp.float32))
        return (mixed / total[..., None]).astype(jnp.bfloat16)

    latent_result = lax.map(one_request, (query_latent, query_rotary, latent_cache, rope_cache, new_latent, key_new, lengths))
    return jnp.einsum('ufia,iaj->ufij', latent_result.astype(jnp.float32), value_up_matrix.astype(jnp.float32)).astype(jnp.bfloat16)
```

```python
import jax
import jax.numpy as jnp
from jax import lax
from jax.experimental import pallas as pl
from jax.experimental.pallas import tpu as pltpu
from jax.sharding import PartitionSpec as P


BLOCK = 1024
NEG_FILL = -1e30
LANES = 128


def rotate(vectors, where_at):
    half_width = vectors.shape[-1] // 2
    frequency = 10000.0 ** (-jnp.arange(half_width, dtype=jnp.float32) / half_width)
    angles = where_at.astype(jnp.float32)[..., None] * frequency
    leading = vectors[..., :half_width].astype(jnp.float32)
    trailing = vectors[..., half_width:].astype(jnp.float32)
    return jnp.concatenate(
        [
            leading * jnp.cos(angles) - trailing * jnp.sin(angles),
            leading * jnp.sin(angles) + trailing * jnp.cos(angles),
        ],
        axis=-1,
    )


def vmem():
    return pl.BlockSpec(memory_space=pltpu.VMEM)


def smem():
    return pl.BlockSpec(memory_space=pltpu.SMEM)


def row_iota(shape):
    return lax.broadcasted_iota(jnp.int32, shape, 0)


def lane_iota(shape):
    return lax.broadcasted_iota(jnp.int32, shape, 1)


def project_queries(query_nope, query_rope, key_absorb):
    groups, steps, heads, nope = query_nope.shape
    latent = key_absorb.shape[2]
    rope = query_rope.shape[2] // heads
    rows = steps * heads
    width = groups * latent + max(groups * rope, LANES)

    def body(nope_ref, rope_ref, absorb_ref, out_ref):
        flat = nope_ref[...]
        head_of = row_iota(flat.shape) % heads
        left = jnp.concatenate([jnp.where(head_of == h, flat, jnp.zeros_like(flat)) for h in range(heads)], axis=1)
        found = jnp.dot(left, absorb_ref[...], preferred_element_type=jnp.float32)
        for g in range(groups):
            out_ref[:, g * latent : (g + 1) * latent] = found[g * rows : (g + 1) * rows].astype(jnp.bfloat16)
        wide = heads * rope
        rows_of = row_iota((rows, wide))
        own_lane = rows_of % heads == lane_iota((rows, wide)) // rope
        parts = []
        for g in range(groups):
            spread = jnp.zeros((rows, wide), jnp.float32)
            for s in range(steps):
                line = rope_ref[g, s : s + 1, :].astype(jnp.float32)
                spread = jnp.where(own_lane & (rows_of // heads == s), line, spread)
            parts.append(spread.astype(jnp.bfloat16))
        tail = width - groups * latent
        picked = jnp.zeros((rows, tail), jnp.float32)
        for g in range(groups):
            choose = (row_iota((wide, tail)) % rope + g * rope == lane_iota((wide, tail))).astype(jnp.float32)
            picked = picked + jnp.dot(parts[g], choose.astype(jnp.bfloat16), preferred_element_type=jnp.float32)
        out_ref[:, groups * latent :] = picked.astype(jnp.bfloat16)

    return pl.pallas_call(
        body,
        in_specs=[vmem(), vmem(), vmem()],
        out_specs=vmem(),
        out_shape=jax.ShapeDtypeStruct((rows, width), jnp.bfloat16),
        name="project_queries",
    )(query_nope.reshape(groups * rows, nope), query_rope, key_absorb.reshape(heads * nope, latent))


def split_stat(stat):
    high = stat.astype(jnp.bfloat16).astype(jnp.float32)
    rest = stat - high
    middle = rest.astype(jnp.bfloat16).astype(jnp.float32)
    return high, middle, rest - middle


def put_stats(stats, shape):
    lanes = lane_iota(shape)
    out = jnp.zeros(shape, jnp.float32)
    for g, stat in enumerate(stats):
        for i, piece in enumerate(split_stat(stat)):
            out = jnp.where(lanes == 3 * g + i, piece, out)
    return out.astype(jnp.bfloat16)


def get_stat(tile, g):
    return jnp.sum(jnp.where(lane_iota(tile.shape) // 3 == g, tile, 0.0), axis=1, keepdims=True)


def attend(pieces, latent_cache, rope_cache, live, rope, softmax_scale):
    groups, keys, latent = latent_cache.shape
    sizes = [piece.shape[0] for piece in pieces]
    rows, width = sum(sizes), pieces[0].shape[1]
    block = min(BLOCK, keys)

    def body(live_ref, latent_ref, rope_ref, *refs):
        queries = refs[: len(pieces)]
        outs = refs[len(pieces) : 2 * len(pieces)]
        query_ref, turned_ref, sum_ref = refs[2 * len(pieces) :]
        stats = []
        for g in range(groups):
            at = 0
            for ref, size in zip(queries, sizes):
                query_ref[at : at + size] = ref[:, g * latent : (g + 1) * latent]
                start = groups * latent + g * rope
                turned_ref[at : at + size] = ref[:, start : start + rope]
                at += size
            count = live_ref[g]
            sum_ref[...] = jnp.zeros_like(sum_ref)

            def step(j, state, g=g, count=count):
                top, total = state
                first = pl.multiple_of(j * block, block)
                held = latent_ref[g, pl.ds(first, block), :]
                score = lax.dot_general(
                    query_ref[...], held, (((1,), (1,)), ((), ())), preferred_element_type=jnp.float32
                )
                score = score + jnp.dot(
                    turned_ref[...], rope_ref[g, :, pl.ds(first, block)], preferred_element_type=jnp.float32
                )
                score = score * softmax_scale
                score = jnp.where(first + lane_iota(score.shape) < count, score, NEG_FILL)
                peak = jnp.maximum(top, jnp.max(score, axis=1, keepdims=True))
                shrink = jnp.exp(top - peak)
                weight = jnp.exp(score - peak)
                sum_ref[...] = sum_ref[...] * shrink + jnp.dot(
                    weight.astype(jnp.bfloat16), held, preferred_element_type=jnp.float32
                )
                return peak, total * shrink + jnp.sum(weight, axis=1, keepdims=True)

            top, total = lax.fori_loop(
                0,
                (count + block - 1) // block,
                step,
                (jnp.full((rows, 1), NEG_FILL, jnp.float32), jnp.zeros((rows, 1), jnp.float32)),
            )
            some = total > 0.0
            safe = jnp.where(some, total, 1.0)
            mean = (sum_ref[...] / safe).astype(jnp.bfloat16)
            stats.append(jnp.where(some, top + jnp.log(safe), NEG_FILL))
            at = 0
            for ref, size in zip(outs, sizes):
                ref[:, g * latent : (g + 1) * latent] = mean[at : at + size]
                at += size
        tile = put_stats(stats, (rows, width - groups * latent))
        at = 0
        for ref, size in zip(outs, sizes):
            ref[:, groups * latent :] = tile[at : at + size]
            at += size

    return pl.pallas_call(
        body,
        in_specs=[smem(), vmem(), vmem()] + [vmem()] * len(pieces),
        out_specs=[vmem()] * len(pieces),
        out_shape=[jax.ShapeDtypeStruct((size, width), jnp.bfloat16) for size in sizes],
        scratch_shapes=[
            pltpu.VMEM((rows, latent), jnp.bfloat16),
            pltpu.VMEM((rows, rope), jnp.bfloat16),
            pltpu.VMEM((rows, latent), jnp.float32),
        ],
        name="attend",
    )(live, latent_cache, rope_cache, *pieces)


def merge_means(pieces, groups, latent):
    rows, width = pieces[0].shape

    def body(*refs):
        ins, out_ref = refs[:-1], refs[-1]
        tiles = [ref[:, groups * latent :].astype(jnp.float32) for ref in ins]
        stats = []
        for g in range(groups):
            logs = [get_stat(tile, g) for tile in tiles]
            top = logs[0]
            for log in logs[1:]:
                top = jnp.maximum(top, log)
            weights = [jnp.exp(log - top) for log in logs]
            total = sum(weights)
            mean = sum(
                ref[:, g * latent : (g + 1) * latent].astype(jnp.float32) * (weight / total)
                for ref, weight in zip(ins, weights)
            )
            out_ref[:, g * latent : (g + 1) * latent] = mean.astype(jnp.bfloat16)
            stats.append(top + jnp.log(total))
        out_ref[:, groups * latent :] = put_stats(stats, (rows, width - groups * latent))

    return pl.pallas_call(
        body,
        in_specs=[vmem()] * len(pieces),
        out_specs=vmem(),
        out_shape=jax.ShapeDtypeStruct((rows, width), jnp.bfloat16),
        name="merge_means",
    )(*pieces)


def finish(pieces, queries, new_latent, key_new, value_up, softmax_scale):
    groups, steps, latent = new_latent.shape
    heads, _, wide = value_up.shape
    rope = key_new.shape[2]
    rows = steps * heads

    def body(*refs):
        ins = refs[: len(pieces)]
        query_ref, new_ref, key_ref, up_ref, out_ref = refs[len(pieces) :]
        tiles = [ref[:, groups * latent :].astype(jnp.float32) for ref in ins]
        step_of = row_iota((rows, 1)) // heads
        results = []
        for g in range(groups):
            logs = [get_stat(tile, g) for tile in tiles]
            start = groups * latent + g * rope
            own = query_ref[:, g * latent : (g + 1) * latent].astype(jnp.float32)
            turned = query_ref[:, start : start + rope].astype(jnp.float32)
            news = [new_ref[g, j : j + 1, :].astype(jnp.float32) for j in range(steps)]
            scores = []
            for j in range(steps):
                key = key_ref[g, j : j + 1, :].astype(jnp.float32)
                score = jnp.sum(own * news[j], axis=1, keepdims=True) + jnp.sum(turned * key, axis=1, keepdims=True)
                scores.append(jnp.where(step_of >= j, score * softmax_scale, NEG_FILL))
            top = scores[0]
            for other in scores[1:] + logs:
                top = jnp.maximum(top, other)
            parts = [jnp.exp(log - top) for log in logs]
            weights = [jnp.where(step_of >= j, jnp.exp(scores[j] - top), 0.0) for j in range(steps)]
            total = sum(parts) + sum(weights)
            mixed = sum(ref[:, g * latent : (g + 1) * latent].astype(jnp.float32) * part for ref, part in zip(ins, parts))
            mixed = mixed + sum(weights[j].astype(jnp.bfloat16).astype(jnp.float32) * news[j] for j in range(steps))
            results.append((mixed / total).astype(jnp.bfloat16))
        mean = jnp.concatenate(results, axis=0)
        head_of = row_iota((groups * rows, wide)) % heads
        picked = jnp.zeros((groups * rows, wide), jnp.float32)
        for h in range(heads):
            picked = jnp.where(head_of == h, jnp.dot(mean, up_ref[h], preferred_element_type=jnp.float32), picked)
        out_ref[...] = picked.astype(jnp.bfloat16)

    return pl.pallas_call(
        body,
        in_specs=[vmem()] * (len(pieces) + 4),
        out_specs=vmem(),
        out_shape=jax.ShapeDtypeStruct((groups * rows, wide), jnp.bfloat16),
        name="finish",
    )(*pieces, queries, new_latent, key_new, value_up)


def on_device(shards):
    near = 4 if shards % 4 == 0 else shards
    nears = range(1, near)
    fars = range(near, shards, near)

    def send(piece, offset):
        return lax.ppermute(piece, "seq", [(i, i ^ offset) for i in range(shards)])

    def program(
        query_nope,
        query_rope,
        key_absorb,
        value_up_matrix,
        latent_cache,
        rope_cache,
        new_latent,
        new_rope,
        lengths,
        positions,
    ):
        groups, steps, heads, nope = query_nope.shape
        latent = key_absorb.shape[2]
        rope = new_rope.shape[2]
        keys = latent_cache.shape[1]
        softmax_scale = (nope + rope) ** (-0.5)
        own = project_queries(query_nope, query_rope, key_absorb)
        rows = own.shape[0]
        got = {0: own}
        for far in fars:
            got[far] = send(own, far)
        for offset in nears:
            got[offset] = send(own, offset)
        for far in fars:
            for offset in nears:
                got[far ^ offset] = send(got[far], offset)
        live = jnp.clip(lengths - lax.axis_index("seq") * keys, 0, keys)
        pieces = [got[k] for k in range(shards)]
        if rows % 16 == 0:
            means = attend(pieces, latent_cache, rope_cache, live, rope, softmax_scale)
        else:
            whole = attend([jnp.concatenate(pieces)], latent_cache, rope_cache, live, rope, softmax_scale)[0]
            means = [whole[k * rows : (k + 1) * rows] for k in range(shards)]
        came = {}
        for far in fars:
            for offset in nears:
                came[far, offset] = send(means[far ^ offset], offset)
        last = [means[0]] + [send(means[offset], offset) for offset in nears]
        for far in fars:
            merged = merge_means([means[far]] + [came[far, offset] for offset in nears], groups, latent)
            last.append(send(merged, far))
        key_new = rotate(new_rope, positions).astype(jnp.bfloat16)
        out = finish(last, own, new_latent, key_new, value_up_matrix, softmax_scale)
        return out.reshape(groups, steps, heads, value_up_matrix.shape[2])

    return program


def solution(mesh):
    return jax.shard_map(
        on_device(mesh.shape["seq"]),
        mesh=mesh,
        in_specs=(
            P("req", None, "seq", None),
            P("req", None, "seq"),
            P("seq", None, None),
            P("seq", None, None),
            P("req", "seq", None),
            P("req", None, "seq"),
            P("req", None, None),
            P("req", None, None),
            P("req"),
            P("req", None),
        ),
        out_specs=P("req", None, "seq", None),
        check_vma=False,
    )
```

```python
import jax
import jax.numpy as jnp
import numpy as np
from jax import lax
from jax.experimental import pallas as pl
from jax.experimental.pallas import tpu as pltpu
from jax.sharding import PartitionSpec as P


BLOCK = 1024
NEG_FILL = -1e30
LANES = 128
LOG2_E = 1.4426950408889634


def vmem():
    return pl.BlockSpec(memory_space=pltpu.VMEM)


def hbm():
    return pl.BlockSpec(memory_space=pltpu.HBM)


def far_core(array):
    return pltpu.with_memory_space_constraint(array, pltpu.HBM)


def near_core(array):
    return pltpu.with_memory_space_constraint(array, pltpu.VMEM)


def smem():
    return pl.BlockSpec(memory_space=pltpu.SMEM)


def row_iota(shape):
    return lax.broadcasted_iota(jnp.int32, shape, 0)


def lane_iota(shape):
    return lax.broadcasted_iota(jnp.int32, shape, 1)


def project_queries(query_nope, query_rope, key_absorb):
    groups, steps, heads, nope = query_nope.shape
    latent = key_absorb.shape[2]
    rope = query_rope.shape[2] // heads
    rows = steps * heads
    width = groups * latent + max(groups * rope, LANES)

    parts = heads if heads < 4 else 4
    share = heads // parts * nope

    def body(nope_hbm, rope_hbm, absorb_hbm, out_ref, nope_ref, rope_ref, absorb_ref, sems):
        copies = [
            pltpu.make_async_copy(nope_hbm, nope_ref, sems.at[parts]),
            pltpu.make_async_copy(rope_hbm, rope_ref, sems.at[parts + 1]),
        ]
        chunks = [
            pltpu.make_async_copy(
                absorb_hbm.at[c * share : (c + 1) * share], absorb_ref.at[c * share : (c + 1) * share], sems.at[c]
            )
            for c in range(parts)
        ]
        for copy in copies + chunks:
            copy.start()
        wide = heads * rope
        tail = width - groups * latent
        rows_of = row_iota((rows, wide))
        own_lane = rows_of % heads == lane_iota((rows, wide)) // rope
        copies[1].wait()
        picked = jnp.zeros((rows, tail), jnp.float32)
        for g in range(groups):
            spread = jnp.zeros((rows, wide), jnp.float32)
            for s in range(steps):
                line = rope_ref[g, s : s + 1, :].astype(jnp.float32)
                spread = jnp.where(own_lane & (rows_of // heads == s), line, spread)
            choose = (row_iota((wide, tail)) % rope + g * rope == lane_iota((wide, tail))).astype(jnp.float32)
            picked = picked + jnp.dot(
                spread.astype(jnp.bfloat16), choose.astype(jnp.bfloat16), preferred_element_type=jnp.float32
            )
        out_ref[:, groups * latent :] = picked.astype(jnp.bfloat16)
        copies[0].wait()
        flat = nope_ref[...]
        head_of = row_iota(flat.shape) % heads
        found = None
        for c, chunk in enumerate(chunks):
            each = heads // parts
            left = [jnp.where(head_of == h, flat, jnp.zeros_like(flat)) for h in range(c * each, (c + 1) * each)]
            chunk.wait()
            more = jnp.dot(
                jnp.concatenate(left, axis=1) if each > 1 else left[0],
                absorb_ref[c * share : (c + 1) * share],
                preferred_element_type=jnp.float32,
            )
            found = more if found is None else found + more
        for g in range(groups):
            out_ref[:, g * latent : (g + 1) * latent] = found[g * rows : (g + 1) * rows].astype(jnp.bfloat16)

    return pl.pallas_call(
        body,
        in_specs=[hbm(), hbm(), hbm()],
        out_specs=vmem(),
        out_shape=jax.ShapeDtypeStruct((rows, width), jnp.bfloat16),
        scratch_shapes=[
            pltpu.VMEM((groups * rows, nope), jnp.bfloat16),
            pltpu.VMEM(query_rope.shape, jnp.bfloat16),
            pltpu.VMEM((heads * nope, latent), jnp.bfloat16),
            pltpu.SemaphoreType.DMA((parts + 2,)),
        ],
        name="project_queries",
        compiler_params=pltpu.CompilerParams(vmem_limit_bytes=12 << 20),
    )(
        far_core(query_nope.reshape(groups * rows, nope)),
        far_core(query_rope),
        far_core(key_absorb.reshape(heads * nope, latent)),
    )


def split_stat(stat):
    high = stat.astype(jnp.bfloat16).astype(jnp.float32)
    rest = stat - high
    middle = rest.astype(jnp.bfloat16).astype(jnp.float32)
    return high, middle, rest - middle


def put_stats(stats, shape):
    lanes = lane_iota(shape)
    out = jnp.zeros(shape, jnp.float32)
    for g, stat in enumerate(stats):
        for i, piece in enumerate(split_stat(stat)):
            out = jnp.where(lanes == 3 * g + i, piece, out)
    return out.astype(jnp.bfloat16)


def get_stat(tile, g):
    return jnp.sum(jnp.where(lane_iota(tile.shape) // 3 == g, tile, 0.0), axis=1, keepdims=True)


def load_cache(latent_cache, rope_cache, new_rope, positions, after):
    groups, steps, rope = new_rope.shape
    half = rope // 2
    frequency = np.tile(10000.0 ** (-np.arange(half, dtype=np.float64) / half), 2)[None].astype(np.float32)

    def body(
        position_hbm,
        frequency_hbm,
        new_hbm,
        latent_hbm,
        rope_hbm,
        after_ref,
        latent_ref,
        rope_ref,
        key_ref,
        position_ref,
        frequency_ref,
        new_ref,
        sems,
    ):
        del after_ref
        pairs = [
            (position_hbm, position_ref),
            (frequency_hbm, frequency_ref),
            (new_hbm, new_ref),
            (latent_hbm, latent_ref),
            (rope_hbm, rope_ref),
        ]
        copies = [pltpu.make_async_copy(source, target, sems.at[i]) for i, (source, target) in enumerate(pairs)]
        for copy in copies:
            copy.start()
        for copy in copies[:3]:
            copy.wait()
        for g in range(groups):
            for j in range(steps):
                angles = position_ref[g, j].astype(jnp.float32) * frequency_ref[...]
                vector = new_ref[g, j : j + 1, :].astype(jnp.float32)
                turned = jnp.concatenate([-vector[:, half:], vector[:, :half]], axis=1)
                key = vector * jnp.cos(angles) + turned * jnp.sin(angles)
                key_ref[g, j : j + 1, :] = key.astype(jnp.bfloat16).astype(jnp.float32)
        for copy in copies[3:]:
            copy.wait()

    return pl.pallas_call(
        body,
        in_specs=[hbm()] * 5 + [pl.BlockSpec(memory_space=pl.ANY)],
        out_specs=[vmem(), vmem(), vmem()],
        out_shape=[
            pltpu.VMEM(latent_cache.shape, jnp.bfloat16),
            pltpu.VMEM(rope_cache.shape, jnp.bfloat16),
            jax.ShapeDtypeStruct(new_rope.shape, jnp.float32),
        ],
        scratch_shapes=[
            pltpu.SMEM(positions.shape, jnp.int32),
            pltpu.VMEM(frequency.shape, jnp.float32),
            pltpu.VMEM(new_rope.shape, jnp.bfloat16),
            pltpu.SemaphoreType.DMA((5,)),
        ],
        name="load_cache",
        compiler_params=pltpu.CompilerParams(vmem_limit_bytes=1 << 20),
    )(*[far_core(x) for x in (positions, jnp.asarray(frequency), new_rope, latent_cache, rope_cache)], after)


def attend(pieces, latent_cache, rope_cache, lengths, rope, softmax_scale):
    groups, keys, latent = latent_cache.shape
    sizes = [piece.shape[0] for piece in pieces]
    rows, width = sum(sizes), pieces[0].shape[1]
    block = min(BLOCK, keys)
    scale = softmax_scale * LOG2_E

    def body(length_ref, latent_ref, rope_ref, *refs):
        queries = refs[: len(pieces)]
        outs = refs[len(pieces) : 2 * len(pieces)]
        query_ref, turned_ref, sum_ref, stat_ref = refs[2 * len(pieces) :]
        before = lax.axis_index("seq") * keys
        counts = [jnp.clip(length_ref[g] - before, 0, keys) for g in range(groups)]
        for g in range(groups):
            at = 0
            for ref, size in zip(queries, sizes):
                query_ref[g, at : at + size] = ref[:, g * latent : (g + 1) * latent]
                start = groups * latent + g * rope
                turned_ref[g, at : at + size] = ref[:, start : start + rope]
                at += size

        def part_of(j):
            return pl.ds(j * block if isinstance(j, int) else pl.multiple_of(j * block, block), block)

        def scores(g, j):
            found = lax.dot_general(
                query_ref[g], latent_ref[g, part_of(j), :], (((1,), (1,)), ((), ())), preferred_element_type=jnp.float32
            )
            return found + jnp.dot(turned_ref[g], rope_ref[g, :, part_of(j)], preferred_element_type=jnp.float32)

        def absorb(g, j, score, top, total):
            peak = jnp.maximum(top, jnp.max(score, axis=1, keepdims=True) * scale)
            shrink = jnp.exp2(top - peak)
            weight = jnp.exp2(score * scale - peak)
            total = total * shrink + jnp.sum(weight, axis=1, keepdims=True)
            more = jnp.dot(weight.astype(jnp.bfloat16), latent_ref[g, part_of(j), :], preferred_element_type=jnp.float32)
            return peak, total, shrink, more

        def start_state():
            return jnp.full((rows, 1), NEG_FILL, jnp.float32), jnp.zeros((rows, 1), jnp.float32)

        def put(g, top, total):
            some = total > 0.0
            safe = jnp.where(some, total, 1.0)
            mean = (sum_ref[g] * (1.0 / safe)).astype(jnp.bfloat16)
            at = 0
            for ref, size in zip(outs, sizes):
                ref[:, g * latent : (g + 1) * latent] = mean[at : at + size]
                at += size
            return jnp.where(some, top + jnp.log2(safe), NEG_FILL)

        def put_tile(stats):
            tile = put_stats(stats, (rows, width - groups * latent))
            at = 0
            for ref, size in zip(outs, sizes):
                ref[:, groups * latent :] = tile[at : at + size]
                at += size

        def run(g, blocks):
            if blocks == 0:
                sum_ref[g] = jnp.zeros((rows, latent), jnp.float32)
                return start_state()
            state = start_state()
            ahead = scores(g, 0)
            for j in range(blocks):
                score = ahead
                if j + 1 < blocks:
                    ahead = scores(g, j + 1)
                else:
                    score = jnp.where(j * block + lane_iota(score.shape) < counts[g], score, NEG_FILL)
                top, total, shrink, more = absorb(g, j, score, *state)
                sum_ref[g] = more if j == 0 else sum_ref[g] * shrink + more
                state = top, total
            return state

        for g in range(groups):
            for blocks in range(keys // block + 1):

                @pl.when((counts[g] + block - 1) // block == blocks)
                def _(g=g, blocks=blocks):
                    stat_ref[g] = jnp.broadcast_to(put(g, *run(g, blocks)), (rows, LANES))

        put_tile([stat_ref[g][:, :1] for g in range(groups)])

    return pl.pallas_call(
        body,
        in_specs=[smem(), vmem(), vmem()] + [vmem()] * len(pieces),
        out_specs=[vmem()] * len(pieces),
        out_shape=[jax.ShapeDtypeStruct((size, width), jnp.bfloat16) for size in sizes],
        scratch_shapes=[
            pltpu.VMEM((groups, rows, latent), jnp.bfloat16),
            pltpu.VMEM((groups, rows, rope), jnp.bfloat16),
            pltpu.VMEM((groups, rows, latent), jnp.float32),
            pltpu.VMEM((groups, rows, LANES), jnp.float32),
        ],
        name="attend",
        compiler_params=pltpu.CompilerParams(vmem_limit_bytes=32 << 20),
    )(lengths, near_core(latent_cache), near_core(rope_cache), *[near_core(p) for p in pieces])


def merge_means(pieces, groups, latent):
    rows, width = pieces[0].shape

    def body(*refs):
        ins, out_ref = refs[:-1], refs[-1]
        tiles = [ref[:, groups * latent :].astype(jnp.float32) for ref in ins]
        stats = []
        for g in range(groups):
            logs = [get_stat(tile, g) for tile in tiles]
            top = logs[0]
            for log in logs[1:]:
                top = jnp.maximum(top, log)
            weights = [jnp.exp2(log - top) for log in logs]
            total = sum(weights)
            mean = sum(
                ref[:, g * latent : (g + 1) * latent].astype(jnp.float32) * (weight / total)
                for ref, weight in zip(ins, weights)
            )
            out_ref[:, g * latent : (g + 1) * latent] = mean.astype(jnp.bfloat16)
            stats.append(top + jnp.log2(total))
        out_ref[:, groups * latent :] = put_stats(stats, (rows, width - groups * latent))

    return pl.pallas_call(
        body,
        in_specs=[vmem()] * len(pieces),
        out_specs=vmem(),
        out_shape=jax.ShapeDtypeStruct((rows, width), jnp.bfloat16),
        name="merge_means",
        compiler_params=pltpu.CompilerParams(vmem_limit_bytes=8 << 20),
    )(*[near_core(p) for p in pieces])


def finish(pieces, queries, new_latent, key_new, value_up, softmax_scale):
    groups, steps, latent = new_latent.shape
    heads, _, wide = value_up.shape
    rope = key_new.shape[2]
    rows = steps * heads

    def body(*refs):
        ins = refs[: len(pieces)]
        query_ref, new_ref, key_ref, up_ref, out_ref = refs[len(pieces) :]
        tiles = [ref[:, groups * latent :].astype(jnp.float32) for ref in ins]
        step_of = row_iota((rows, 1)) // heads
        results = []
        for g in range(groups):
            logs = [get_stat(tile, g) for tile in tiles]
            start = groups * latent + g * rope
            own = query_ref[:, g * latent : (g + 1) * latent].astype(jnp.float32)
            turned = query_ref[:, start : start + rope].astype(jnp.float32)
            news = [new_ref[g, j : j + 1, :].astype(jnp.float32) for j in range(steps)]
            scores = []
            for j in range(steps):
                key = key_ref[g, j : j + 1, :]
                score = jnp.sum(own * news[j], axis=1, keepdims=True) + jnp.sum(turned * key, axis=1, keepdims=True)
                scores.append(jnp.where(step_of >= j, score * (softmax_scale * LOG2_E), NEG_FILL))
            top = scores[0]
            for other in scores[1:] + logs:
                top = jnp.maximum(top, other)
            parts = [jnp.exp2(log - top) for log in logs]
            weights = [jnp.where(step_of >= j, jnp.exp2(scores[j] - top), 0.0) for j in range(steps)]
            total = sum(parts) + sum(weights)
            mixed = sum(ref[:, g * latent : (g + 1) * latent].astype(jnp.float32) * part for ref, part in zip(ins, parts))
            mixed = mixed + sum(weights[j].astype(jnp.bfloat16).astype(jnp.float32) * news[j] for j in range(steps))
            results.append((mixed * (1.0 / total)).astype(jnp.bfloat16))
        mean = jnp.concatenate(results, axis=0)
        head_of = row_iota((groups * rows, wide)) % heads
        picked = jnp.zeros((groups * rows, wide), jnp.float32)
        for h in range(heads):
            picked = jnp.where(head_of == h, jnp.dot(mean, up_ref[h], preferred_element_type=jnp.float32), picked)
        out_ref[...] = picked.astype(jnp.bfloat16)

    return pl.pallas_call(
        body,
        in_specs=[vmem()] * (len(pieces) + 4),
        out_specs=vmem(),
        out_shape=jax.ShapeDtypeStruct((groups * rows, wide), jnp.bfloat16),
        name="finish",
        compiler_params=pltpu.CompilerParams(vmem_limit_bytes=12 << 20),
    )(*[near_core(p) for p in pieces], near_core(queries), new_latent, key_new, near_core(value_up))


def on_device(shards):
    near = 4 if shards % 4 == 0 else shards
    nears = range(1, near)
    fars = range(near, shards, near)

    def send(piece, offset):
        return lax.ppermute(piece, "seq", [(i, i ^ offset) for i in range(shards)])

    def program(
        query_nope,
        query_rope,
        key_absorb,
        value_up_matrix,
        latent_cache,
        rope_cache,
        new_latent,
        new_rope,
        lengths,
        positions,
    ):
        groups, steps, heads, nope = query_nope.shape
        latent = key_absorb.shape[2]
        rope = new_rope.shape[2]
        softmax_scale = (nope + rope) ** (-0.5)
        own = project_queries(query_nope, query_rope, key_absorb)
        rows = own.shape[0]
        got = {0: own}
        for far in fars:
            got[far] = send(own, far)
        for offset in nears:
            got[offset] = send(own, offset)
        for far in fars:
            for offset in nears:
                got[far ^ offset] = send(got[far], offset)
        pieces = [got[k] for k in range(shards)]
        latent_cache, rope_cache, key_new = load_cache(
            latent_cache, rope_cache, new_rope, positions, got[near % shards]
        )
        if rows % 16 == 0:
            means = attend(pieces, latent_cache, rope_cache, lengths, rope, softmax_scale)
        else:
            whole = attend([jnp.concatenate(pieces)], latent_cache, rope_cache, lengths, rope, softmax_scale)[0]
            means = [whole[k * rows : (k + 1) * rows] for k in range(shards)]
        came = {}
        for far in fars:
            for offset in nears:
                came[far, offset] = send(means[far ^ offset], offset)
        last = [means[0]] + [send(means[offset], offset) for offset in nears]
        for far in fars:
            merged = merge_means([means[far]] + [came[far, offset] for offset in nears], groups, latent)
            last.append(send(merged, far))
        out = finish(last, own, new_latent, key_new, value_up_matrix, softmax_scale)
        return out.reshape(groups, steps, heads, value_up_matrix.shape[2])

    return program


def solution(mesh):
    return jax.shard_map(
        on_device(mesh.shape["seq"]),
        mesh=mesh,
        in_specs=(
            P("req", None, "seq", None),
            P("req", None, "seq"),
            P("seq", None, None),
            P("seq", None, None),
            P("req", "seq", None),
            P("req", None, "seq"),
            P("req", None, None),
            P("req", None, None),
            P("req"),
            P("req", None),
        ),
        out_specs=P("req", None, "seq", None),
        check_vma=False,
    )
```

```python
import jax
import jax.numpy as jnp
import numpy as np
from jax import lax
from jax.experimental import pallas as pl
from jax.experimental.pallas import tpu as pltpu
from jax.sharding import PartitionSpec as P


BLOCK = 2048
NEG_FILL = -1e30
LANES = 128
JOINED = (3,)
LOG2_E = 1.4426950408889634


def vmem():
    return pl.BlockSpec(memory_space=pltpu.VMEM)


def hbm():
    return pl.BlockSpec(memory_space=pltpu.HBM)


def far_core(array):
    return pltpu.with_memory_space_constraint(array, pltpu.HBM)


def near_core(array):
    return pltpu.with_memory_space_constraint(array, pltpu.VMEM)


def smem():
    return pl.BlockSpec(memory_space=pltpu.SMEM)


def row_iota(shape):
    return lax.broadcasted_iota(jnp.int32, shape, 0)


def lane_iota(shape):
    return lax.broadcasted_iota(jnp.int32, shape, 1)


def project_queries(query_nope, query_rope, key_absorb):
    groups, steps, heads, nope = query_nope.shape
    latent = key_absorb.shape[2]
    rope = query_rope.shape[2] // heads
    rows = steps * heads
    width = groups * latent + max(groups * rope, LANES)

    parts = heads if heads < 4 else 4
    share = heads // parts * nope

    def body(nope_hbm, rope_hbm, absorb_hbm, out_ref, nope_ref, rope_ref, absorb_ref, sems):
        copies = [
            pltpu.make_async_copy(nope_hbm, nope_ref, sems.at[parts]),
            pltpu.make_async_copy(rope_hbm, rope_ref, sems.at[parts + 1]),
        ]
        chunks = [
            pltpu.make_async_copy(
                absorb_hbm.at[c * share : (c + 1) * share], absorb_ref.at[c * share : (c + 1) * share], sems.at[c]
            )
            for c in range(parts)
        ]
        for copy in copies + chunks:
            copy.start()
        wide = heads * rope
        tail = width - groups * latent
        rows_of = row_iota((rows, wide))
        own_lane = rows_of % heads == lane_iota((rows, wide)) // rope
        copies[1].wait()
        picked = jnp.zeros((rows, tail), jnp.float32)
        for g in range(groups):
            spread = jnp.zeros((rows, wide), jnp.float32)
            for s in range(steps):
                line = rope_ref[g, s : s + 1, :].astype(jnp.float32)
                spread = jnp.where(own_lane & (rows_of // heads == s), line, spread)
            choose = (row_iota((wide, tail)) % rope + g * rope == lane_iota((wide, tail))).astype(jnp.float32)
            picked = picked + jnp.dot(
                spread.astype(jnp.bfloat16), choose.astype(jnp.bfloat16), preferred_element_type=jnp.float32
            )
        out_ref[:, groups * latent :] = picked.astype(jnp.bfloat16)
        copies[0].wait()
        flat = nope_ref[...]
        head_of = row_iota(flat.shape) % heads
        found = None
        for c, chunk in enumerate(chunks):
            each = heads // parts
            left = [jnp.where(head_of == h, flat, jnp.zeros_like(flat)) for h in range(c * each, (c + 1) * each)]
            chunk.wait()
            more = jnp.dot(
                jnp.concatenate(left, axis=1) if each > 1 else left[0],
                absorb_ref[c * share : (c + 1) * share],
                preferred_element_type=jnp.float32,
            )
            found = more if found is None else found + more
        for g in range(groups):
            out_ref[:, g * latent : (g + 1) * latent] = found[g * rows : (g + 1) * rows].astype(jnp.bfloat16)

    return pl.pallas_call(
        body,
        in_specs=[hbm(), hbm(), hbm()],
        out_specs=vmem(),
        out_shape=jax.ShapeDtypeStruct((rows, width), jnp.bfloat16),
        scratch_shapes=[
            pltpu.VMEM((groups * rows, nope), jnp.bfloat16),
            pltpu.VMEM(query_rope.shape, jnp.bfloat16),
            pltpu.VMEM((heads * nope, latent), jnp.bfloat16),
            pltpu.SemaphoreType.DMA((parts + 2,)),
        ],
        name="project_queries",
        compiler_params=pltpu.CompilerParams(vmem_limit_bytes=12 << 20),
    )(
        far_core(query_nope.reshape(groups * rows, nope)),
        far_core(query_rope),
        far_core(key_absorb.reshape(heads * nope, latent)),
    )


def split_stat(stat):
    high = stat.astype(jnp.bfloat16).astype(jnp.float32)
    rest = stat - high
    middle = rest.astype(jnp.bfloat16).astype(jnp.float32)
    return high, middle, rest - middle


def put_stats(stats, shape):
    lanes = lane_iota(shape)
    out = jnp.zeros(shape, jnp.float32)
    for g, stat in enumerate(stats):
        for i, piece in enumerate(split_stat(stat)):
            out = jnp.where(lanes == 3 * g + i, piece, out)
    return out.astype(jnp.bfloat16)


def get_stat(tile, g):
    return jnp.sum(jnp.where(lane_iota(tile.shape) // 3 == g, tile, 0.0), axis=1, keepdims=True)


def load_cache(latent_cache, rope_cache, new_rope, positions, after):
    groups, steps, rope = new_rope.shape
    half = rope // 2
    frequency = np.tile(10000.0 ** (-np.arange(half, dtype=np.float64) / half), 2)[None].astype(np.float32)

    def body(
        position_hbm,
        frequency_hbm,
        new_hbm,
        latent_hbm,
        rope_hbm,
        after_ref,
        latent_ref,
        rope_ref,
        key_ref,
        position_ref,
        frequency_ref,
        new_ref,
        sems,
    ):
        del after_ref
        pairs = [
            (position_hbm, position_ref),
            (frequency_hbm, frequency_ref),
            (new_hbm, new_ref),
            (latent_hbm, latent_ref),
            (rope_hbm, rope_ref),
        ]
        copies = [pltpu.make_async_copy(source, target, sems.at[i]) for i, (source, target) in enumerate(pairs)]
        for copy in copies:
            copy.start()
        for copy in copies[:3]:
            copy.wait()
        for g in range(groups):
            for j in range(steps):
                angles = position_ref[g, j].astype(jnp.float32) * frequency_ref[...]
                vector = new_ref[g, j : j + 1, :].astype(jnp.float32)
                turned = jnp.concatenate([-vector[:, half:], vector[:, :half]], axis=1)
                key = vector * jnp.cos(angles) + turned * jnp.sin(angles)
                key_ref[g, j : j + 1, :] = key.astype(jnp.bfloat16).astype(jnp.float32)
        for copy in copies[3:]:
            copy.wait()

    return pl.pallas_call(
        body,
        in_specs=[hbm()] * 5 + [pl.BlockSpec(memory_space=pl.ANY)],
        out_specs=[vmem(), vmem(), vmem()],
        out_shape=[
            pltpu.VMEM(latent_cache.shape, jnp.bfloat16),
            pltpu.VMEM(rope_cache.shape, jnp.bfloat16),
            jax.ShapeDtypeStruct(new_rope.shape, jnp.float32),
        ],
        scratch_shapes=[
            pltpu.SMEM(positions.shape, jnp.int32),
            pltpu.VMEM(frequency.shape, jnp.float32),
            pltpu.VMEM(new_rope.shape, jnp.bfloat16),
            pltpu.SemaphoreType.DMA((5,)),
        ],
        name="load_cache",
        compiler_params=pltpu.CompilerParams(vmem_limit_bytes=1 << 20),
    )(*[far_core(x) for x in (positions, jnp.asarray(frequency), new_rope, latent_cache, rope_cache)], after)


def attend(pieces, together, latent_cache, rope_cache, lengths, rope, softmax_scale):
    groups, keys, latent = latent_cache.shape
    sizes = [piece.shape[0] for piece in pieces]
    rows, width = sum(sizes), pieces[0].shape[1]
    block = min(BLOCK, keys)
    scale = softmax_scale * LOG2_E
    starts = [sum(sizes[:i]) for i in range(len(sizes))]

    def body(length_ref, latent_ref, rope_ref, *refs):
        queries = refs[: len(pieces)]
        outs = refs[len(pieces) : len(pieces) + len(together)]
        turned_ref, sum_ref, stat_ref = refs[len(pieces) + len(together) :]
        before = lax.axis_index("seq") * keys
        for g in range(groups):
            at = 0
            for ref, size in zip(queries, sizes):
                start = groups * latent + g * rope
                turned_ref[g, at : at + size] = ref[:, start : start + rope]
                at += size

        def part_of(j):
            return pl.ds(j * block if isinstance(j, int) else pl.multiple_of(j * block, block), block)

        def scores(g, j):
            mine = pl.ds(pl.multiple_of(g * latent, LANES), latent)
            asked = [ref[:, mine] for ref in queries]
            found = lax.dot_general(
                jnp.concatenate(asked) if len(asked) > 1 else asked[0], latent_ref[g, part_of(j), :], (((1,), (1,)), ((), ())), preferred_element_type=jnp.float32
            )
            return found + jnp.dot(turned_ref[g], rope_ref[g, :, part_of(j)], preferred_element_type=jnp.float32)

        def absorb(g, j, score, top, total):
            peak = jnp.maximum(top, jnp.max(score, axis=1, keepdims=True) * scale)
            shrink = jnp.exp2(top - peak)
            weight = jnp.exp2(score * scale - peak)
            total = total * shrink + jnp.sum(weight, axis=1, keepdims=True)
            more = jnp.dot(weight.astype(jnp.bfloat16), latent_ref[g, part_of(j), :], preferred_element_type=jnp.float32)
            return peak, total, shrink, more

        def start_state():
            return jnp.full((rows, 1), NEG_FILL, jnp.float32), jnp.zeros((rows, 1), jnp.float32)

        def put(g, top, total):
            some = total > 0.0
            safe = jnp.where(some, total, 1.0)
            mean = (sum_ref[g] * (1.0 / safe)).astype(jnp.bfloat16)
            for ref, chunks in zip(outs, together):
                at = 0
                for c in chunks:
                    lanes = pl.ds(pl.multiple_of(g * latent, LANES), latent)
                    ref[at : at + sizes[c], lanes] = mean[starts[c] : starts[c] + sizes[c]]
                    at += sizes[c]
            return jnp.where(some, top + jnp.log2(safe), NEG_FILL)

        def put_tile(stats):
            tile = put_stats(stats, (rows, width - groups * latent))
            for ref, chunks in zip(outs, together):
                at = 0
                for c in chunks:
                    ref[at : at + sizes[c], groups * latent :] = tile[starts[c] : starts[c] + sizes[c]]
                    at += sizes[c]

        def run(g, count, blocks):
            if blocks == 0:
                sum_ref[g] = jnp.zeros((rows, latent), jnp.float32)
                return start_state()
            state = start_state()
            ahead = scores(g, 0)
            for j in range(blocks):
                score = ahead
                if j + 1 < blocks:
                    ahead = scores(g, j + 1)
                else:
                    score = jnp.where(j * block + lane_iota(score.shape) < count, score, NEG_FILL)
                top, total, shrink, more = absorb(g, j, score, *state)
                sum_ref[g] = more if j == 0 else sum_ref[g] * shrink + more
                state = top, total
            return state

        @pl.loop(0, groups)
        def _(g):
            count = jnp.clip(length_ref[g] - before, 0, keys)
            for blocks in range(keys // block + 1):

                @pl.when((count + block - 1) // block == blocks)
                def _(blocks=blocks):
                    stat_ref[g] = jnp.broadcast_to(put(g, *run(g, count, blocks)), (rows, LANES))

        put_tile([stat_ref[g][:, :1] for g in range(groups)])

    return pl.pallas_call(
        body,
        in_specs=[smem(), vmem(), vmem()] + [vmem()] * len(pieces),
        out_specs=[vmem()] * len(together),
        out_shape=[
            jax.ShapeDtypeStruct((sum(sizes[c] for c in chunks), width), jnp.bfloat16) for chunks in together
        ],
        scratch_shapes=[
            pltpu.VMEM((groups, rows, rope), jnp.bfloat16),
            pltpu.VMEM((groups, rows, latent), jnp.float32),
            pltpu.VMEM((groups, rows, LANES), jnp.float32),
        ],
        name="attend",
        compiler_params=pltpu.CompilerParams(vmem_limit_bytes=32 << 20),
    )(lengths, near_core(latent_cache), near_core(rope_cache), *[near_core(p) for p in pieces])


def merge_means(pieces, rows, groups, latent):
    width = pieces[0][0].shape[1]

    def body(*refs):
        ins, out_ref = [ref.at[at : at + rows] for ref, (_, at) in zip(refs, pieces)], refs[-1]
        tiles = [ref[:, groups * latent :].astype(jnp.float32) for ref in ins]
        stats = []
        for g in range(groups):
            logs = [get_stat(tile, g) for tile in tiles]
            top = logs[0]
            for log in logs[1:]:
                top = jnp.maximum(top, log)
            weights = [jnp.exp2(log - top) for log in logs]
            total = sum(weights)
            mean = sum(
                ref[:, g * latent : (g + 1) * latent].astype(jnp.float32) * (weight / total)
                for ref, weight in zip(ins, weights)
            )
            out_ref[:, g * latent : (g + 1) * latent] = mean.astype(jnp.bfloat16)
            stats.append(top + jnp.log2(total))
        out_ref[:, groups * latent :] = put_stats(stats, (rows, width - groups * latent))

    return pl.pallas_call(
        body,
        in_specs=[vmem()] * len(pieces),
        out_specs=vmem(),
        out_shape=jax.ShapeDtypeStruct((rows, width), jnp.bfloat16),
        name="merge_means",
        compiler_params=pltpu.CompilerParams(vmem_limit_bytes=8 << 20),
    )(*[near_core(p) for p, _ in pieces])


def finish(pieces, queries, new_latent, key_new, value_up, softmax_scale):
    groups, steps, latent = new_latent.shape
    heads, _, wide = value_up.shape
    rope = key_new.shape[2]
    rows = steps * heads
    pair = 2 if heads % 2 == 0 else 1

    def body(*refs):
        ins = [ref.at[at : at + rows] for ref, (_, at) in zip(refs, pieces)]
        query_ref, new_ref, key_ref, up_ref, out_ref = refs[len(pieces) :]
        tiles = [ref[:, groups * latent :].astype(jnp.float32) for ref in ins]
        step_of = row_iota((rows, 1)) // heads
        results = []
        for g in range(groups):
            logs = [get_stat(tile, g) for tile in tiles]
            start = groups * latent + g * rope
            own = query_ref[:, g * latent : (g + 1) * latent].astype(jnp.float32)
            turned = query_ref[:, start : start + rope].astype(jnp.float32)
            news = [new_ref[g, j : j + 1, :].astype(jnp.float32) for j in range(steps)]
            scores = []
            for j in range(steps):
                key = key_ref[g, j : j + 1, :]
                score = jnp.sum(own * news[j], axis=1, keepdims=True) + jnp.sum(turned * key, axis=1, keepdims=True)
                scores.append(jnp.where(step_of >= j, score * (softmax_scale * LOG2_E), NEG_FILL))
            top = scores[0]
            for other in scores[1:] + logs:
                top = jnp.maximum(top, other)
            parts = [jnp.exp2(log - top) for log in logs]
            weights = [jnp.where(step_of >= j, jnp.exp2(scores[j] - top), 0.0) for j in range(steps)]
            total = sum(parts) + sum(weights)
            mixed = sum(ref[:, g * latent : (g + 1) * latent].astype(jnp.float32) * part for ref, part in zip(ins, parts))
            mixed = mixed + sum(weights[j].astype(jnp.bfloat16).astype(jnp.float32) * news[j] for j in range(steps))
            results.append((mixed * (1.0 / total)).astype(jnp.bfloat16))
        mean = jnp.concatenate(results, axis=0)
        head_of = row_iota((groups * rows, wide)) % heads
        picked = jnp.zeros((groups * rows, wide), jnp.float32)
        for h in range(0, heads, pair):
            beside = jnp.concatenate([up_ref[h + i] for i in range(pair)], axis=1)
            found = jnp.dot(mean, beside, preferred_element_type=jnp.float32)
            for i in range(pair):
                picked = jnp.where(head_of == h + i, found[:, i * wide : (i + 1) * wide], picked)
        out_ref[...] = picked.astype(jnp.bfloat16)

    return pl.pallas_call(
        body,
        in_specs=[vmem()] * (len(pieces) + 4),
        out_specs=vmem(),
        out_shape=jax.ShapeDtypeStruct((groups * rows, wide), jnp.bfloat16),
        name="finish",
        compiler_params=pltpu.CompilerParams(vmem_limit_bytes=12 << 20),
    )(*[near_core(p) for p, _ in pieces], near_core(queries), new_latent, key_new, near_core(value_up))


def on_device(shards):
    near = 4 if shards % 4 == 0 else shards
    nears = range(1, near)
    fars = range(near, shards, near)

    def send(piece, offset):
        return lax.ppermute(piece, "seq", [(i, i ^ offset) for i in range(shards)])

    def program(
        query_nope,
        query_rope,
        key_absorb,
        value_up_matrix,
        latent_cache,
        rope_cache,
        new_latent,
        new_rope,
        lengths,
        positions,
    ):
        groups, steps, heads, nope = query_nope.shape
        latent = key_absorb.shape[2]
        rope = new_rope.shape[2]
        softmax_scale = (nope + rope) ** (-0.5)
        own = project_queries(query_nope, query_rope, key_absorb)
        rows = own.shape[0]
        got = {0: own}
        for far in fars:
            got[far] = send(own, far)
        for offset in nears:
            got[offset] = send(own, offset)
        for far in fars:
            for offset in nears:
                got[far ^ offset] = send(got[far], offset)
        pieces = [got[k] for k in range(shards)]
        latent_cache, rope_cache, key_new = load_cache(
            latent_cache, rope_cache, new_rope, positions, got[near % shards]
        )
        first = near % shards
        joined = [offset for offset in JOINED if first and offset < near]
        together = [[first ^ offset, offset] if offset in joined else [first ^ offset] for offset in reversed(nears)]
        together += [[c] for c in range(shards) if all(c not in chunks for chunks in together)]
        if rows % 16 == 0:
            means = attend(pieces, together, latent_cache, rope_cache, lengths, rope, softmax_scale)
        else:
            whole = attend(
                [jnp.concatenate(pieces)], [[0]], latent_cache, rope_cache, lengths, rope, softmax_scale
            )[0]
            means = [jnp.concatenate([whole[c * rows : (c + 1) * rows] for c in chunks]) for chunks in together]
        found = {tuple(chunks): mean for chunks, mean in zip(together, means)}
        place = {c: (chunks, i * rows) for chunks in found for i, c in enumerate(chunks)}
        came = {}

        def receive(chunk, offset):
            chunks, at = place[chunk]
            if chunks not in came:
                came[chunks] = send(found[chunks], offset)
            return came[chunks], at

        def own_part(chunk):
            chunks, at = place[chunk]
            return found[chunks], at

        sides = {far: [receive(far ^ offset, offset) for offset in reversed(nears)] for far in fars}
        last = [own_part(0)] + [receive(offset, offset) for offset in nears]
        for far in fars:
            merged = merge_means([own_part(far)] + sides[far], rows, groups, latent)
            last.append((send(merged, far), 0))
        out = finish(last, own, new_latent, key_new, value_up_matrix, softmax_scale)
        return out.reshape(groups, steps, heads, value_up_matrix.shape[2])

    return program


def solution(mesh):
    return jax.shard_map(
        on_device(mesh.shape["seq"]),
        mesh=mesh,
        in_specs=(
            P("req", None, "seq", None),
            P("req", None, "seq"),
            P("seq", None, None),
            P("seq", None, None),
            P("req", "seq", None),
            P("req", None, "seq"),
            P("req", None, None),
            P("req", None, None),
            P("req"),
            P("req", None),
        ),
        out_specs=P("req", None, "seq", None),
        check_vma=False,
    )
```

```python
import jax
import jax.numpy as jnp
import numpy as np
from jax import lax
from jax.experimental import pallas as pl
from jax.experimental.pallas import tpu as pltpu
from jax.sharding import PartitionSpec as P


BLOCK = 2048
NEG_FILL = -1e30
LANES = 128
JOINED = ()
LOG2_E = 1.4426950408889634


def vmem():
    return pl.BlockSpec(memory_space=pltpu.VMEM)


def hbm():
    return pl.BlockSpec(memory_space=pltpu.HBM)


def far_core(array):
    return pltpu.with_memory_space_constraint(array, pltpu.HBM)


def near_core(array):
    return pltpu.with_memory_space_constraint(array, pltpu.VMEM)


def smem():
    return pl.BlockSpec(memory_space=pltpu.SMEM)


def row_iota(shape):
    return lax.broadcasted_iota(jnp.int32, shape, 0)


def lane_iota(shape):
    return lax.broadcasted_iota(jnp.int32, shape, 1)


def project_queries(query_nope, query_rope, key_absorb):
    groups, steps, heads, nope = query_nope.shape
    latent = key_absorb.shape[2]
    rope = query_rope.shape[2] // heads
    rows = steps * heads
    width = groups * latent + max(groups * rope, LANES)

    parts = heads if heads < 4 else 4
    share = heads // parts * nope

    def body(nope_hbm, rope_hbm, absorb_hbm, out_ref, nope_ref, rope_ref, absorb_ref, sems):
        copies = [
            pltpu.make_async_copy(nope_hbm, nope_ref, sems.at[parts]),
            pltpu.make_async_copy(rope_hbm, rope_ref, sems.at[parts + 1]),
        ]
        chunks = [
            pltpu.make_async_copy(
                absorb_hbm.at[c * share : (c + 1) * share], absorb_ref.at[c * share : (c + 1) * share], sems.at[c]
            )
            for c in range(parts)
        ]
        for copy in copies + chunks:
            copy.start()
        wide = heads * rope
        tail = width - groups * latent
        rows_of = row_iota((rows, wide))
        own_lane = rows_of % heads == lane_iota((rows, wide)) // rope
        copies[1].wait()
        picked = jnp.zeros((rows, tail), jnp.float32)
        for g in range(groups):
            spread = jnp.zeros((rows, wide), jnp.float32)
            for s in range(steps):
                line = rope_ref[g, s : s + 1, :].astype(jnp.float32)
                spread = jnp.where(own_lane & (rows_of // heads == s), line, spread)
            choose = (row_iota((wide, tail)) % rope + g * rope == lane_iota((wide, tail))).astype(jnp.float32)
            picked = picked + jnp.dot(
                spread.astype(jnp.bfloat16), choose.astype(jnp.bfloat16), preferred_element_type=jnp.float32
            )
        out_ref[:, groups * latent :] = picked.astype(jnp.bfloat16)
        copies[0].wait()
        flat = nope_ref[...]
        head_of = row_iota(flat.shape) % heads
        found = None
        for c, chunk in enumerate(chunks):
            each = heads // parts
            left = [jnp.where(head_of == h, flat, jnp.zeros_like(flat)) for h in range(c * each, (c + 1) * each)]
            chunk.wait()
            more = jnp.dot(
                jnp.concatenate(left, axis=1) if each > 1 else left[0],
                absorb_ref[c * share : (c + 1) * share],
                preferred_element_type=jnp.float32,
            )
            found = more if found is None else found + more
        for g in range(groups):
            out_ref[:, g * latent : (g + 1) * latent] = found[g * rows : (g + 1) * rows].astype(jnp.bfloat16)

    return pl.pallas_call(
        body,
        in_specs=[hbm(), hbm(), hbm()],
        out_specs=vmem(),
        out_shape=jax.ShapeDtypeStruct((rows, width), jnp.bfloat16),
        scratch_shapes=[
            pltpu.VMEM((groups * rows, nope), jnp.bfloat16),
            pltpu.VMEM(query_rope.shape, jnp.bfloat16),
            pltpu.VMEM((heads * nope, latent), jnp.bfloat16),
            pltpu.SemaphoreType.DMA((parts + 2,)),
        ],
        name="project_queries",
        compiler_params=pltpu.CompilerParams(vmem_limit_bytes=12 << 20),
    )(
        far_core(query_nope.reshape(groups * rows, nope)),
        far_core(query_rope),
        far_core(key_absorb.reshape(heads * nope, latent)),
    )


def split_stat(stat):
    high = stat.astype(jnp.bfloat16).astype(jnp.float32)
    rest = stat - high
    middle = rest.astype(jnp.bfloat16).astype(jnp.float32)
    return high, middle, rest - middle


def put_stats(stats, shape):
    lanes = lane_iota(shape)
    out = jnp.zeros(shape, jnp.float32)
    for g, stat in enumerate(stats):
        for i, piece in enumerate(split_stat(stat)):
            out = jnp.where(lanes == 3 * g + i, piece, out)
    return out.astype(jnp.bfloat16)


def get_stat(tile, g):
    return jnp.sum(jnp.where(lane_iota(tile.shape) // 3 == g, tile, 0.0), axis=1, keepdims=True)


def load_cache(latent_cache, rope_cache, new_rope, positions, after):
    groups, steps, rope = new_rope.shape
    half = rope // 2
    frequency = np.tile(10000.0 ** (-np.arange(half, dtype=np.float64) / half), 2)[None].astype(np.float32)

    def body(
        position_hbm,
        frequency_hbm,
        new_hbm,
        latent_hbm,
        rope_hbm,
        after_ref,
        latent_ref,
        rope_ref,
        key_ref,
        position_ref,
        frequency_ref,
        new_ref,
        sems,
    ):
        del after_ref
        pairs = [
            (position_hbm, position_ref),
            (frequency_hbm, frequency_ref),
            (new_hbm, new_ref),
            (latent_hbm, latent_ref),
            (rope_hbm, rope_ref),
        ]
        copies = [pltpu.make_async_copy(source, target, sems.at[i]) for i, (source, target) in enumerate(pairs)]
        for copy in copies:
            copy.start()
        for copy in copies[:3]:
            copy.wait()
        for g in range(groups):
            for j in range(steps):
                angles = position_ref[g, j].astype(jnp.float32) * frequency_ref[...]
                vector = new_ref[g, j : j + 1, :].astype(jnp.float32)
                turned = jnp.concatenate([-vector[:, half:], vector[:, :half]], axis=1)
                key = vector * jnp.cos(angles) + turned * jnp.sin(angles)
                key_ref[g, j : j + 1, :] = key.astype(jnp.bfloat16).astype(jnp.float32)
        for copy in copies[3:]:
            copy.wait()

    return pl.pallas_call(
        body,
        in_specs=[hbm()] * 5 + [pl.BlockSpec(memory_space=pl.ANY)],
        out_specs=[vmem(), vmem(), vmem()],
        out_shape=[
            pltpu.VMEM(latent_cache.shape, jnp.bfloat16),
            pltpu.VMEM(rope_cache.shape, jnp.bfloat16),
            jax.ShapeDtypeStruct(new_rope.shape, jnp.float32),
        ],
        scratch_shapes=[
            pltpu.SMEM(positions.shape, jnp.int32),
            pltpu.VMEM(frequency.shape, jnp.float32),
            pltpu.VMEM(new_rope.shape, jnp.bfloat16),
            pltpu.SemaphoreType.DMA((5,)),
        ],
        name="load_cache",
        compiler_params=pltpu.CompilerParams(vmem_limit_bytes=1 << 20),
    )(*[far_core(x) for x in (positions, jnp.asarray(frequency), new_rope, latent_cache, rope_cache)], after)


def attend(pieces, together, latent_cache, rope_cache, lengths, rope, softmax_scale):
    groups, keys, latent = latent_cache.shape
    sizes = [piece.shape[0] for piece in pieces]
    rows, width = sum(sizes), pieces[0].shape[1]
    block = min(BLOCK, keys)
    scale = softmax_scale * LOG2_E
    starts = [sum(sizes[:i]) for i in range(len(sizes))]

    def body(length_ref, latent_ref, rope_ref, *refs):
        queries = refs[: len(pieces)]
        outs = refs[len(pieces) : len(pieces) + len(together)]
        turned_ref, sum_ref, stat_ref = refs[len(pieces) + len(together) :]
        before = lax.axis_index("seq") * keys
        for g in range(groups):
            at = 0
            for ref, size in zip(queries, sizes):
                start = groups * latent + g * rope
                turned_ref[g, at : at + size] = ref[:, start : start + rope]
                at += size

        def part_of(j):
            return pl.ds(j * block if isinstance(j, int) else pl.multiple_of(j * block, block), block)

        def scores(g, j):
            mine = pl.ds(pl.multiple_of(g * latent, LANES), latent)
            asked = [ref[:, mine] for ref in queries]
            found = lax.dot_general(
                jnp.concatenate(asked) if len(asked) > 1 else asked[0], latent_ref[g, part_of(j), :], (((1,), (1,)), ((), ())), preferred_element_type=jnp.float32
            )
            return found + jnp.dot(turned_ref[g], rope_ref[g, :, part_of(j)], preferred_element_type=jnp.float32)

        def absorb(g, j, score, top, total):
            peak = jnp.maximum(top, jnp.max(score, axis=1, keepdims=True) * scale)
            shrink = jnp.exp2(top - peak)
            weight = jnp.exp2(score * scale - peak)
            total = total * shrink + jnp.sum(weight, axis=1, keepdims=True)
            more = jnp.dot(weight.astype(jnp.bfloat16), latent_ref[g, part_of(j), :], preferred_element_type=jnp.float32)
            return peak, total, shrink, more

        def start_state():
            return jnp.full((rows, 1), NEG_FILL, jnp.float32), jnp.zeros((rows, 1), jnp.float32)

        def put(g, top, total):
            some = total > 0.0
            safe = jnp.where(some, total, 1.0)
            mean = (sum_ref[g] * (1.0 / safe)).astype(jnp.bfloat16)
            for ref, chunks in zip(outs, together):
                at = 0
                for c in chunks:
                    lanes = pl.ds(pl.multiple_of(g * latent, LANES), latent)
                    ref[at : at + sizes[c], lanes] = mean[starts[c] : starts[c] + sizes[c]]
                    at += sizes[c]
            return jnp.where(some, top + jnp.log2(safe), NEG_FILL)

        def put_tile(stats):
            tile = put_stats(stats, (rows, width - groups * latent))
            for ref, chunks in zip(outs, together):
                at = 0
                for c in chunks:
                    ref[at : at + sizes[c], groups * latent :] = tile[starts[c] : starts[c] + sizes[c]]
                    at += sizes[c]

        def run(g, count, blocks):
            if blocks == 0:
                sum_ref[g] = jnp.zeros((rows, latent), jnp.float32)
                return start_state()
            state = start_state()
            ahead = scores(g, 0)
            for j in range(blocks):
                score = ahead
                if j + 1 < blocks:
                    ahead = scores(g, j + 1)
                else:
                    score = jnp.where(j * block + lane_iota(score.shape) < count, score, NEG_FILL)
                top, total, shrink, more = absorb(g, j, score, *state)
                sum_ref[g] = more if j == 0 else sum_ref[g] * shrink + more
                state = top, total
            return state

        @pl.loop(0, groups)
        def _(g):
            count = jnp.clip(length_ref[g] - before, 0, keys)
            for blocks in range(keys // block + 1):

                @pl.when((count + block - 1) // block == blocks)
                def _(blocks=blocks):
                    stat_ref[g] = jnp.broadcast_to(put(g, *run(g, count, blocks)), (rows, LANES))

        put_tile([stat_ref[g][:, :1] for g in range(groups)])

    return pl.pallas_call(
        body,
        in_specs=[smem(), vmem(), vmem()] + [vmem()] * len(pieces),
        out_specs=[vmem()] * len(together),
        out_shape=[
            jax.ShapeDtypeStruct((sum(sizes[c] for c in chunks), width), jnp.bfloat16) for chunks in together
        ],
        scratch_shapes=[
            pltpu.VMEM((groups, rows, rope), jnp.bfloat16),
            pltpu.VMEM((groups, rows, latent), jnp.float32),
            pltpu.VMEM((groups, rows, LANES), jnp.float32),
        ],
        name="attend",
        compiler_params=pltpu.CompilerParams(vmem_limit_bytes=32 << 20),
    )(lengths, near_core(latent_cache), near_core(rope_cache), *[near_core(p) for p in pieces])


def merge_means(pieces, rows, groups, latent):
    width = pieces[0][0].shape[1]

    def body(*refs):
        ins, out_ref = [ref.at[at : at + rows] for ref, (_, at) in zip(refs, pieces)], refs[-1]
        tiles = [ref[:, groups * latent :].astype(jnp.float32) for ref in ins]
        stats = []
        for g in range(groups):
            logs = [get_stat(tile, g) for tile in tiles]
            top = logs[0]
            for log in logs[1:]:
                top = jnp.maximum(top, log)
            weights = [jnp.exp2(log - top) for log in logs]
            total = sum(weights)
            mean = sum(
                ref[:, g * latent : (g + 1) * latent].astype(jnp.float32) * (weight / total)
                for ref, weight in zip(ins, weights)
            )
            out_ref[:, g * latent : (g + 1) * latent] = mean.astype(jnp.bfloat16)
            stats.append(top + jnp.log2(total))
        out_ref[:, groups * latent :] = put_stats(stats, (rows, width - groups * latent))

    return pl.pallas_call(
        body,
        in_specs=[vmem()] * len(pieces),
        out_specs=vmem(),
        out_shape=jax.ShapeDtypeStruct((rows, width), jnp.bfloat16),
        name="merge_means",
        compiler_params=pltpu.CompilerParams(vmem_limit_bytes=8 << 20),
    )(*[near_core(p) for p, _ in pieces])


def finish(pieces, queries, new_latent, key_new, value_up, softmax_scale):
    groups, steps, latent = new_latent.shape
    heads, _, wide = value_up.shape
    rope = key_new.shape[2]
    rows = steps * heads
    pair = 2 if heads % 2 == 0 else 1

    def body(*refs):
        ins = [ref.at[at : at + rows] for ref, (_, at) in zip(refs, pieces)]
        query_ref, new_ref, key_ref, up_ref, out_ref = refs[len(pieces) :]
        tiles = [ref[:, groups * latent :].astype(jnp.float32) for ref in ins]
        step_of = row_iota((rows, 1)) // heads
        results = []
        for g in range(groups):
            logs = [get_stat(tile, g) for tile in tiles]
            start = groups * latent + g * rope
            own = query_ref[:, g * latent : (g + 1) * latent].astype(jnp.float32)
            turned = query_ref[:, start : start + rope].astype(jnp.float32)
            news = [new_ref[g, j : j + 1, :].astype(jnp.float32) for j in range(steps)]
            scores = []
            for j in range(steps):
                key = key_ref[g, j : j + 1, :]
                score = jnp.sum(own * news[j], axis=1, keepdims=True) + jnp.sum(turned * key, axis=1, keepdims=True)
                scores.append(jnp.where(step_of >= j, score * (softmax_scale * LOG2_E), NEG_FILL))
            top = scores[0]
            for other in scores[1:] + logs:
                top = jnp.maximum(top, other)
            parts = [jnp.exp2(log - top) for log in logs]
            weights = [jnp.where(step_of >= j, jnp.exp2(scores[j] - top), 0.0) for j in range(steps)]
            total = sum(parts) + sum(weights)
            mixed = sum(ref[:, g * latent : (g + 1) * latent].astype(jnp.float32) * part for ref, part in zip(ins, parts))
            mixed = mixed + sum(weights[j].astype(jnp.bfloat16).astype(jnp.float32) * news[j] for j in range(steps))
            results.append((mixed * (1.0 / total)).astype(jnp.bfloat16))
        mean = jnp.concatenate(results, axis=0)
        head_of = row_iota((groups * rows, wide)) % heads
        picked = jnp.zeros((groups * rows, wide), jnp.float32)
        for h in range(0, heads, pair):
            beside = jnp.concatenate([up_ref[h + i] for i in range(pair)], axis=1)
            found = jnp.dot(mean, beside, preferred_element_type=jnp.float32)
            for i in range(pair):
                picked = jnp.where(head_of == h + i, found[:, i * wide : (i + 1) * wide], picked)
        out_ref[...] = picked.astype(jnp.bfloat16)

    return pl.pallas_call(
        body,
        in_specs=[vmem()] * (len(pieces) + 4),
        out_specs=vmem(),
        out_shape=jax.ShapeDtypeStruct((groups * rows, wide), jnp.bfloat16),
        name="finish",
        compiler_params=pltpu.CompilerParams(vmem_limit_bytes=12 << 20),
    )(*[near_core(p) for p, _ in pieces], near_core(queries), new_latent, key_new, near_core(value_up))


def on_device(shards):
    near = 4 if shards % 4 == 0 else shards
    nears = range(1, near)
    fars = range(near, shards, near)

    def send(piece, offset):
        return lax.ppermute(piece, "seq", [(i, i ^ offset) for i in range(shards)])

    def program(
        query_nope,
        query_rope,
        key_absorb,
        value_up_matrix,
        latent_cache,
        rope_cache,
        new_latent,
        new_rope,
        lengths,
        positions,
    ):
        groups, steps, heads, nope = query_nope.shape
        latent = key_absorb.shape[2]
        rope = new_rope.shape[2]
        softmax_scale = (nope + rope) ** (-0.5)
        own = project_queries(query_nope, query_rope, key_absorb)
        rows = own.shape[0]
        got = {0: own}
        for far in fars:
            got[far] = send(own, far)
        for offset in nears:
            got[offset] = send(own, offset)
        for far in fars:
            for offset in nears:
                got[far ^ offset] = send(got[far], offset)
        pieces = [got[k] for k in range(shards)]
        latent_cache, rope_cache, key_new = load_cache(
            latent_cache, rope_cache, new_rope, positions, got[near % shards]
        )
        first = near % shards
        joined = [offset for offset in JOINED if first and offset < near]
        together = [[first ^ offset, offset] if offset in joined else [first ^ offset] for offset in reversed(nears)]
        together += [[c] for c in range(shards) if all(c not in chunks for chunks in together)]
        if rows % 16 == 0:
            means = attend(pieces, together, latent_cache, rope_cache, lengths, rope, softmax_scale)
        else:
            whole = attend(
                [jnp.concatenate(pieces)], [[0]], latent_cache, rope_cache, lengths, rope, softmax_scale
            )[0]
            means = [jnp.concatenate([whole[c * rows : (c + 1) * rows] for c in chunks]) for chunks in together]
        found = {tuple(chunks): mean for chunks, mean in zip(together, means)}
        place = {c: (chunks, i * rows) for chunks in found for i, c in enumerate(chunks)}
        came = {}

        def receive(chunk, offset):
            chunks, at = place[chunk]
            if chunks not in came:
                came[chunks] = send(found[chunks], offset)
            return came[chunks], at

        def own_part(chunk):
            chunks, at = place[chunk]
            return found[chunks], at

        sides = {far: [receive(far ^ offset, offset) for offset in reversed(nears)] for far in fars}
        last = [own_part(0)] + [receive(offset, offset) for offset in reversed(nears)]
        for far in fars:
            merged = merge_means([own_part(far)] + sides[far], rows, groups, latent)
            last.append((send(merged, far), 0))
        out = finish(last, own, new_latent, key_new, value_up_matrix, softmax_scale)
        return out.reshape(groups, steps, heads, value_up_matrix.shape[2])

    return program


def solution(mesh):
    return jax.shard_map(
        on_device(mesh.shape["seq"]),
        mesh=mesh,
        in_specs=(
            P("req", None, "seq", None),
            P("req", None, "seq"),
            P("seq", None, None),
            P("seq", None, None),
            P("req", "seq", None),
            P("req", None, "seq"),
            P("req", None, None),
            P("req", None, None),
            P("req"),
            P("req", None),
        ),
        out_specs=P("req", None, "seq", None),
        check_vma=False,
    )
```

```python
import jax
import jax.numpy as jnp
import numpy as np
from jax import lax
from jax.experimental import pallas as pl
from jax.experimental.pallas import tpu as pltpu
from jax.sharding import PartitionSpec as P


BLOCK = 2048
NEG_FILL = -1e30
LANES = 128
JOINED = (3,)
ORDER = (2, 3, 1)
LOG2_E = 1.4426950408889634


def vmem():
    return pl.BlockSpec(memory_space=pltpu.VMEM)


def hbm():
    return pl.BlockSpec(memory_space=pltpu.HBM)


def far_core(array):
    return pltpu.with_memory_space_constraint(array, pltpu.HBM)


def near_core(array):
    return pltpu.with_memory_space_constraint(array, pltpu.VMEM)


def smem():
    return pl.BlockSpec(memory_space=pltpu.SMEM)


def row_iota(shape):
    return lax.broadcasted_iota(jnp.int32, shape, 0)


def lane_iota(shape):
    return lax.broadcasted_iota(jnp.int32, shape, 1)


def project_queries(query_nope, query_rope, key_absorb):
    groups, steps, heads, nope = query_nope.shape
    latent = key_absorb.shape[2]
    rope = query_rope.shape[2] // heads
    rows = steps * heads
    width = groups * latent + max(groups * rope, LANES)

    parts = heads if heads < 4 else 4
    share = heads // parts * nope

    def body(nope_hbm, rope_hbm, absorb_hbm, out_ref, nope_ref, rope_ref, absorb_ref, sems):
        copies = [
            pltpu.make_async_copy(nope_hbm, nope_ref, sems.at[parts]),
            pltpu.make_async_copy(rope_hbm, rope_ref, sems.at[parts + 1]),
        ]
        chunks = [
            pltpu.make_async_copy(
                absorb_hbm.at[c * share : (c + 1) * share], absorb_ref.at[c * share : (c + 1) * share], sems.at[c]
            )
            for c in range(parts)
        ]
        for copy in copies + chunks:
            copy.start()
        wide = heads * rope
        tail = width - groups * latent
        rows_of = row_iota((rows, wide))
        own_lane = rows_of % heads == lane_iota((rows, wide)) // rope
        copies[1].wait()
        picked = jnp.zeros((rows, tail), jnp.float32)
        for g in range(groups):
            spread = jnp.zeros((rows, wide), jnp.float32)
            for s in range(steps):
                line = rope_ref[g, s : s + 1, :].astype(jnp.float32)
                spread = jnp.where(own_lane & (rows_of // heads == s), line, spread)
            choose = (row_iota((wide, tail)) % rope + g * rope == lane_iota((wide, tail))).astype(jnp.float32)
            picked = picked + jnp.dot(
                spread.astype(jnp.bfloat16), choose.astype(jnp.bfloat16), preferred_element_type=jnp.float32
            )
        out_ref[:, groups * latent :] = picked.astype(jnp.bfloat16)
        copies[0].wait()
        flat = nope_ref[...]
        head_of = row_iota(flat.shape) % heads
        found = None
        for c, chunk in enumerate(chunks):
            each = heads // parts
            left = [jnp.where(head_of == h, flat, jnp.zeros_like(flat)) for h in range(c * each, (c + 1) * each)]
            chunk.wait()
            more = jnp.dot(
                jnp.concatenate(left, axis=1) if each > 1 else left[0],
                absorb_ref[c * share : (c + 1) * share],
                preferred_element_type=jnp.float32,
            )
            found = more if found is None else found + more
        for g in range(groups):
            out_ref[:, g * latent : (g + 1) * latent] = found[g * rows : (g + 1) * rows].astype(jnp.bfloat16)

    return pl.pallas_call(
        body,
        in_specs=[hbm(), hbm(), hbm()],
        out_specs=vmem(),
        out_shape=jax.ShapeDtypeStruct((rows, width), jnp.bfloat16),
        scratch_shapes=[
            pltpu.VMEM((groups * rows, nope), jnp.bfloat16),
            pltpu.VMEM(query_rope.shape, jnp.bfloat16),
            pltpu.VMEM((heads * nope, latent), jnp.bfloat16),
            pltpu.SemaphoreType.DMA((parts + 2,)),
        ],
        name="project_queries",
        compiler_params=pltpu.CompilerParams(vmem_limit_bytes=12 << 20),
    )(
        far_core(query_nope.reshape(groups * rows, nope)),
        far_core(query_rope),
        far_core(key_absorb.reshape(heads * nope, latent)),
    )


def split_stat(stat):
    high = stat.astype(jnp.bfloat16).astype(jnp.float32)
    rest = stat - high
    middle = rest.astype(jnp.bfloat16).astype(jnp.float32)
    return high, middle, rest - middle


def put_stats(stats, shape):
    lanes = lane_iota(shape)
    out = jnp.zeros(shape, jnp.float32)
    for g, stat in enumerate(stats):
        for i, piece in enumerate(split_stat(stat)):
            out = jnp.where(lanes == 3 * g + i, piece, out)
    return out.astype(jnp.bfloat16)


def get_stat(tile, g):
    return jnp.sum(jnp.where(lane_iota(tile.shape) // 3 == g, tile, 0.0), axis=1, keepdims=True)


def load_cache(latent_cache, rope_cache, new_rope, positions, after):
    groups, steps, rope = new_rope.shape
    half = rope // 2
    frequency = np.tile(10000.0 ** (-np.arange(half, dtype=np.float64) / half), 2)[None].astype(np.float32)

    def body(
        position_hbm,
        frequency_hbm,
        new_hbm,
        latent_hbm,
        rope_hbm,
        after_ref,
        latent_ref,
        rope_ref,
        key_ref,
        position_ref,
        frequency_ref,
        new_ref,
        sems,
    ):
        del after_ref
        pairs = [
            (position_hbm, position_ref),
            (frequency_hbm, frequency_ref),
            (new_hbm, new_ref),
            (latent_hbm, latent_ref),
            (rope_hbm, rope_ref),
        ]
        copies = [pltpu.make_async_copy(source, target, sems.at[i]) for i, (source, target) in enumerate(pairs)]
        for copy in copies:
            copy.start()
        for copy in copies[:3]:
            copy.wait()
        for g in range(groups):
            for j in range(steps):
                angles = position_ref[g, j].astype(jnp.float32) * frequency_ref[...]
                vector = new_ref[g, j : j + 1, :].astype(jnp.float32)
                turned = jnp.concatenate([-vector[:, half:], vector[:, :half]], axis=1)
                key = vector * jnp.cos(angles) + turned * jnp.sin(angles)
                key_ref[g, j : j + 1, :] = key.astype(jnp.bfloat16).astype(jnp.float32)
        for copy in copies[3:]:
            copy.wait()

    return pl.pallas_call(
        body,
        in_specs=[hbm()] * 5 + [pl.BlockSpec(memory_space=pl.ANY)],
        out_specs=[vmem(), vmem(), vmem()],
        out_shape=[
            pltpu.VMEM(latent_cache.shape, jnp.bfloat16),
            pltpu.VMEM(rope_cache.shape, jnp.bfloat16),
            jax.ShapeDtypeStruct(new_rope.shape, jnp.float32),
        ],
        scratch_shapes=[
            pltpu.SMEM(positions.shape, jnp.int32),
            pltpu.VMEM(frequency.shape, jnp.float32),
            pltpu.VMEM(new_rope.shape, jnp.bfloat16),
            pltpu.SemaphoreType.DMA((5,)),
        ],
        name="load_cache",
        compiler_params=pltpu.CompilerParams(vmem_limit_bytes=1 << 20),
    )(*[far_core(x) for x in (positions, jnp.asarray(frequency), new_rope, latent_cache, rope_cache)], after)


def attend(pieces, together, latent_cache, rope_cache, lengths, rope, softmax_scale):
    groups, keys, latent = latent_cache.shape
    sizes = [piece.shape[0] for piece in pieces]
    rows, width = sum(sizes), pieces[0].shape[1]
    block = min(BLOCK, keys)
    scale = softmax_scale * LOG2_E
    starts = [sum(sizes[:i]) for i in range(len(sizes))]

    def body(length_ref, latent_ref, rope_ref, *refs):
        queries = refs[: len(pieces)]
        outs = refs[len(pieces) : len(pieces) + len(together)]
        turned_ref, sum_ref, stat_ref = refs[len(pieces) + len(together) :]
        before = lax.axis_index("seq") * keys
        for g in range(groups):
            at = 0
            for ref, size in zip(queries, sizes):
                start = groups * latent + g * rope
                turned_ref[g, at : at + size] = ref[:, start : start + rope]
                at += size

        def part_of(j):
            return pl.ds(j * block if isinstance(j, int) else pl.multiple_of(j * block, block), block)

        def scores(g, j):
            mine = pl.ds(pl.multiple_of(g * latent, LANES), latent)
            asked = [ref[:, mine] for ref in queries]
            found = lax.dot_general(
                jnp.concatenate(asked) if len(asked) > 1 else asked[0], latent_ref[g, part_of(j), :], (((1,), (1,)), ((), ())), preferred_element_type=jnp.float32
            )
            return found + jnp.dot(turned_ref[g], rope_ref[g, :, part_of(j)], preferred_element_type=jnp.float32)

        def absorb(g, j, score, top, total):
            peak = jnp.maximum(top, jnp.max(score, axis=1, keepdims=True) * scale)
            shrink = jnp.exp2(top - peak)
            weight = jnp.exp2(score * scale - peak)
            total = total * shrink + jnp.sum(weight, axis=1, keepdims=True)
            more = jnp.dot(weight.astype(jnp.bfloat16), latent_ref[g, part_of(j), :], preferred_element_type=jnp.float32)
            return peak, total, shrink, more

        def start_state():
            return jnp.full((rows, 1), NEG_FILL, jnp.float32), jnp.zeros((rows, 1), jnp.float32)

        def put(g, top, total):
            some = total > 0.0
            safe = jnp.where(some, total, 1.0)
            mean = (sum_ref[g] * (1.0 / safe)).astype(jnp.bfloat16)
            for ref, chunks in zip(outs, together):
                at = 0
                for c in chunks:
                    lanes = pl.ds(pl.multiple_of(g * latent, LANES), latent)
                    ref[at : at + sizes[c], lanes] = mean[starts[c] : starts[c] + sizes[c]]
                    at += sizes[c]
            return jnp.where(some, top + jnp.log2(safe), NEG_FILL)

        def put_tile(stats):
            tile = put_stats(stats, (rows, width - groups * latent))
            for ref, chunks in zip(outs, together):
                at = 0
                for c in chunks:
                    ref[at : at + sizes[c], groups * latent :] = tile[starts[c] : starts[c] + sizes[c]]
                    at += sizes[c]

        def run(g, count, blocks):
            if blocks == 0:
                sum_ref[g] = jnp.zeros((rows, latent), jnp.float32)
                return start_state()
            state = start_state()
            ahead = scores(g, 0)
            for j in range(blocks):
                score = ahead
                if j + 1 < blocks:
                    ahead = scores(g, j + 1)
                else:
                    score = jnp.where(j * block + lane_iota(score.shape) < count, score, NEG_FILL)
                top, total, shrink, more = absorb(g, j, score, *state)
                sum_ref[g] = more if j == 0 else sum_ref[g] * shrink + more
                state = top, total
            return state

        @pl.loop(0, groups)
        def _(g):
            count = jnp.clip(length_ref[g] - before, 0, keys)
            for blocks in range(keys // block + 1):

                @pl.when((count + block - 1) // block == blocks)
                def _(blocks=blocks):
                    stat_ref[g] = jnp.broadcast_to(put(g, *run(g, count, blocks)), (rows, LANES))

        put_tile([stat_ref[g][:, :1] for g in range(groups)])

    return pl.pallas_call(
        body,
        in_specs=[smem(), vmem(), vmem()] + [vmem()] * len(pieces),
        out_specs=[vmem()] * len(together),
        out_shape=[
            jax.ShapeDtypeStruct((sum(sizes[c] for c in chunks), width), jnp.bfloat16) for chunks in together
        ],
        scratch_shapes=[
            pltpu.VMEM((groups, rows, rope), jnp.bfloat16),
            pltpu.VMEM((groups, rows, latent), jnp.float32),
            pltpu.VMEM((groups, rows, LANES), jnp.float32),
        ],
        name="attend",
        compiler_params=pltpu.CompilerParams(vmem_limit_bytes=32 << 20),
    )(lengths, near_core(latent_cache), near_core(rope_cache), *[near_core(p) for p in pieces])


def merge_means(pieces, rows, groups, latent):
    width = pieces[0][0].shape[1]

    def body(*refs):
        ins, out_ref = [ref.at[at : at + rows] for ref, (_, at) in zip(refs, pieces)], refs[-1]
        tiles = [ref[:, groups * latent :].astype(jnp.float32) for ref in ins]
        stats = []
        for g in range(groups):
            logs = [get_stat(tile, g) for tile in tiles]
            top = logs[0]
            for log in logs[1:]:
                top = jnp.maximum(top, log)
            weights = [jnp.exp2(log - top) for log in logs]
            total = sum(weights)
            mean = sum(
                ref[:, g * latent : (g + 1) * latent].astype(jnp.float32) * (weight / total)
                for ref, weight in zip(ins, weights)
            )
            out_ref[:, g * latent : (g + 1) * latent] = mean.astype(jnp.bfloat16)
            stats.append(top + jnp.log2(total))
        out_ref[:, groups * latent :] = put_stats(stats, (rows, width - groups * latent))

    return pl.pallas_call(
        body,
        in_specs=[vmem()] * len(pieces),
        out_specs=vmem(),
        out_shape=jax.ShapeDtypeStruct((rows, width), jnp.bfloat16),
        name="merge_means",
        compiler_params=pltpu.CompilerParams(vmem_limit_bytes=8 << 20),
    )(*[near_core(p) for p, _ in pieces])


def finish(pieces, queries, new_latent, key_new, value_up, softmax_scale):
    groups, steps, latent = new_latent.shape
    heads, _, wide = value_up.shape
    rope = key_new.shape[2]
    rows = steps * heads
    pair = 2 if heads % 2 == 0 else 1

    def body(*refs):
        ins = [ref.at[at : at + rows] for ref, (_, at) in zip(refs, pieces)]
        query_ref, new_ref, key_ref, up_ref, out_ref = refs[len(pieces) :]
        tiles = [ref[:, groups * latent :].astype(jnp.float32) for ref in ins]
        step_of = row_iota((rows, 1)) // heads
        results = []
        for g in range(groups):
            logs = [get_stat(tile, g) for tile in tiles]
            start = groups * latent + g * rope
            own = query_ref[:, g * latent : (g + 1) * latent].astype(jnp.float32)
            turned = query_ref[:, start : start + rope].astype(jnp.float32)
            news = [new_ref[g, j : j + 1, :].astype(jnp.float32) for j in range(steps)]
            scores = []
            for j in range(steps):
                key = key_ref[g, j : j + 1, :]
                score = jnp.sum(own * news[j], axis=1, keepdims=True) + jnp.sum(turned * key, axis=1, keepdims=True)
                scores.append(jnp.where(step_of >= j, score * (softmax_scale * LOG2_E), NEG_FILL))
            top = scores[0]
            for other in scores[1:] + logs:
                top = jnp.maximum(top, other)
            parts = [jnp.exp2(log - top) for log in logs]
            weights = [jnp.where(step_of >= j, jnp.exp2(scores[j] - top), 0.0) for j in range(steps)]
            total = sum(parts) + sum(weights)
            mixed = sum(ref[:, g * latent : (g + 1) * latent].astype(jnp.float32) * part for ref, part in zip(ins, parts))
            mixed = mixed + sum(weights[j].astype(jnp.bfloat16).astype(jnp.float32) * news[j] for j in range(steps))
            results.append((mixed * (1.0 / total)).astype(jnp.bfloat16))
        mean = jnp.concatenate(results, axis=0)
        head_of = row_iota((groups * rows, wide)) % heads
        picked = jnp.zeros((groups * rows, wide), jnp.float32)
        for h in range(0, heads, pair):
            beside = jnp.concatenate([up_ref[h + i] for i in range(pair)], axis=1)
            found = jnp.dot(mean, beside, preferred_element_type=jnp.float32)
            for i in range(pair):
                picked = jnp.where(head_of == h + i, found[:, i * wide : (i + 1) * wide], picked)
        out_ref[...] = picked.astype(jnp.bfloat16)

    return pl.pallas_call(
        body,
        in_specs=[vmem()] * (len(pieces) + 4),
        out_specs=vmem(),
        out_shape=jax.ShapeDtypeStruct((groups * rows, wide), jnp.bfloat16),
        name="finish",
        compiler_params=pltpu.CompilerParams(vmem_limit_bytes=12 << 20),
    )(*[near_core(p) for p, _ in pieces], near_core(queries), new_latent, key_new, near_core(value_up))


def on_device(shards):
    near = 4 if shards % 4 == 0 else shards
    nears = range(1, near)
    fars = range(near, shards, near)

    def send(piece, offset):
        return lax.ppermute(piece, "seq", [(i, i ^ offset) for i in range(shards)])

    def program(
        query_nope,
        query_rope,
        key_absorb,
        value_up_matrix,
        latent_cache,
        rope_cache,
        new_latent,
        new_rope,
        lengths,
        positions,
    ):
        groups, steps, heads, nope = query_nope.shape
        latent = key_absorb.shape[2]
        rope = new_rope.shape[2]
        softmax_scale = (nope + rope) ** (-0.5)
        own = project_queries(query_nope, query_rope, key_absorb)
        rows = own.shape[0]
        got = {0: own}
        for far in fars:
            got[far] = send(own, far)
        for offset in nears:
            got[offset] = send(own, offset)
        for far in fars:
            for offset in nears:
                got[far ^ offset] = send(got[far], offset)
        pieces = [got[k] for k in range(shards)]
        latent_cache, rope_cache, key_new = load_cache(
            latent_cache, rope_cache, new_rope, positions, got[near % shards]
        )
        first = near % shards
        order = sorted(nears, key=ORDER.index) if near == 4 else nears
        joined = [offset for offset in JOINED if first and offset < near]
        together = [[first ^ offset, offset] if offset in joined else [first ^ offset] for offset in order]
        together += [[c] for c in range(shards) if all(c not in chunks for chunks in together)]
        if rows % 16 == 0:
            means = attend(pieces, together, latent_cache, rope_cache, lengths, rope, softmax_scale)
        else:
            whole = attend(
                [jnp.concatenate(pieces)], [[0]], latent_cache, rope_cache, lengths, rope, softmax_scale
            )[0]
            means = [jnp.concatenate([whole[c * rows : (c + 1) * rows] for c in chunks]) for chunks in together]
        found = {tuple(chunks): mean for chunks, mean in zip(together, means)}
        place = {c: (chunks, i * rows) for chunks in found for i, c in enumerate(chunks)}
        came = {}

        def receive(chunk, offset):
            chunks, at = place[chunk]
            if chunks not in came:
                came[chunks] = send(found[chunks], offset)
            return came[chunks], at

        def own_part(chunk):
            chunks, at = place[chunk]
            return found[chunks], at

        sides = {far: [receive(far ^ offset, offset) for offset in order] for far in fars}
        last = [own_part(0)] + [receive(offset, offset) for offset in order]
        for far in fars:
            merged = merge_means([own_part(far)] + sides[far], rows, groups, latent)
            last.append((send(merged, far), 0))
        out = finish(last, own, new_latent, key_new, value_up_matrix, softmax_scale)
        return out.reshape(groups, steps, heads, value_up_matrix.shape[2])

    return program


def solution(mesh):
    return jax.shard_map(
        on_device(mesh.shape["seq"]),
        mesh=mesh,
        in_specs=(
            P("req", None, "seq", None),
            P("req", None, "seq"),
            P("seq", None, None),
            P("seq", None, None),
            P("req", "seq", None),
            P("req", None, "seq"),
            P("req", None, None),
            P("req", None, None),
            P("req"),
            P("req", None),
        ),
        out_specs=P("req", None, "seq", None),
        check_vma=False,
    )
```
